32 devices in a mesh: row: 4 (over y, x), orb: 8 (over z, core).
Axes of the slice: x: 2, y: 2, z: 4, core: 2. Of those that a mesh axis runs over, the one named last changes fastest.
Arguments:
- integrals: bfloat16 [24, 1024, 5120], P('orb', 'row'), may hold values from -6 to 6
- tile_ids: int32 [8, 40], P('row'), may hold values from 0 to 127, as said below
- coefficients: bfloat16 [1024, 16384], P('orb'), may hold values from -0.078125 to 0.078125
- metric: float32 [24, 24], replicated, may hold values from -0.0078125 to 0.0078125
Outputs:
- exchange_columns: float32 [1024, 1024], P('orb', 'row')
The draws below stay inside these ranges and needn't reach their ends.
Inputs may be any that keep to these rules, and one draw needn't show every extreme that they name: `tile_ids`: row block b covers basis functions b * 128 to b * 128 + 127. Each row lists 40 different column tiles (tile t covers basis functions t * 128 to t * 128 + 127); the first is the block's own tile b.
All inputs are finite; a program needn't handle non-finite values.
Results may differ from the reference program's by a relative error of at most 0.022.
Values may be sent and summed in bfloat16 or wider, within the bound.
A program may use at most 128 MiB of HBM per device.

```python
import jax
import jax.numpy as jnp
from jax import lax

TILE = 128
KEPT = 40
BLK_DEV = 2
NB = 16384
NOCC = 1024
AUX = 24
ROWS = 1024


def draw_tile_ids(key, part):
    blocks = ROWS // TILE
    tile_total = NB // TILE
    random_keys = jax.random.randint(key, (blocks, tile_total), 0, 1 << 20)
    scores = random_keys * tile_total + jnp.arange(tile_total, dtype=jnp.int32)[None, :]
    own_tile = jnp.arange(blocks, dtype=jnp.int32)[:, None] == jnp.arange(tile_total, dtype=jnp.int32)[None, :]
    scores = jnp.where(own_tile, 1 << 30, scores)
    _, chosen = lax.top_k(scores, KEPT)
    return chosen.astype(jnp.int32)


def block_scale(key, extent, split, low, top_value):
    factor_of, own = 1.0, jax.random.fold_in(key, 6)
    for axis_at, shards_of in split:
        steps = jnp.exp(jax.random.uniform(jax.random.fold_in(own, axis_at), (shards_of,), jnp.float32, low / len(split), top_value / len(split)))
        factor_of = factor_of * jnp.repeat(steps, extent[axis_at] // shards_of).reshape([-1 if axis == axis_at else 1 for axis in range(len(extent))])
    return factor_of


def scatter_about(rng, dims, width, reach, split=(), held_as=jnp.bfloat16):
    level = block_scale(rng, dims, split, -0.22, 0.18) if split else 1.0
    values = jax.random.normal(rng, dims, jnp.float32) * width * level
    return jnp.minimum(jnp.maximum(values, -reach), reach).astype(held_as)


def setup_inputs(seed: int = 0) -> dict:
    key_list = jax.random.split(jax.random.key(seed), 5)
    integrals = scatter_about(key_list[0], (AUX, ROWS, KEPT * TILE), 1.0, 6.0, ((0, 8), (1, 4)))
    tile_ids = draw_tile_ids(jax.random.fold_in(key_list[4], 71), 0)
    coefficients = scatter_about(key_list[2], (NOCC, NB), (KEPT * TILE) ** -0.5, 0.078125, ((0, 8),))
    metric = scatter_about(key_list[3], (AUX, AUX), (AUX * AUX * NOCC) ** -0.5, 0.0078125, (), jnp.float32)
    return dict(integrals=integrals, tile_ids=tile_ids, coefficients=coefficients, metric=metric)


def reference(integrals, tile_ids, coefficients, metric):
    group_rows = BLK_DEV * TILE
    groups = ROWS // group_rows
    blocked = coefficients.reshape(NOCC, NB // TILE, TILE)

    def one_group(running, group_index):
        row_slab = lax.dynamic_slice_in_dim(integrals, group_index * group_rows, group_rows, 1)
        row_slab = row_slab.reshape(AUX, BLK_DEV, TILE, KEPT * TILE)
        group_ids = lax.dynamic_slice_in_dim(tile_ids, group_index * BLK_DEV, BLK_DEV, 0)
        picked = jnp.take(blocked, group_ids.reshape(BLK_DEV * KEPT), axis=1).reshape(NOCC, BLK_DEV, KEPT * TILE)
        halves = jnp.einsum("pbmk,jbk->pjbm", row_slab.astype(jnp.float32), picked.astype(jnp.float32))
        halves = halves.reshape(AUX, NOCC, group_rows).astype(jnp.bfloat16)
        halves = lax.optimization_barrier(halves)
        own_rows = lax.dynamic_slice_in_dim(coefficients, group_index * group_rows, group_rows, 1)
        partial_group = jnp.einsum("qjm,im->qji", halves.astype(jnp.float32), own_rows.astype(jnp.float32)).astype(jnp.bfloat16)
        partial_group = lax.optimization_barrier(partial_group)
        return running + partial_group.astype(jnp.float32), halves

    zeros_init = jnp.zeros((AUX, NOCC, NOCC), jnp.float32)
    occupied, halves_all = lax.scan(one_group, zeros_init, jnp.arange(groups, dtype=jnp.int32))
    fitted = jnp.einsum("pq,qji->pji", metric, occupied, precision=lax.Precision.HIGHEST).astype(jnp.bfloat16)
    fitted = lax.optimization_barrier(fitted)
    fitted_wide = fitted.astype(jnp.float32)

    def columns(group_index):
        return jnp.einsum("pjm,pji->im", halves_all[group_index].astype(jnp.float32), fitted_wide)

    column_blocks = lax.map(columns, jnp.arange(groups, dtype=jnp.int32))
    return jnp.transpose(column_blocks, (1, 0, 2)).reshape(NOCC, ROWS)
```

```python
import functools

import jax
import jax.numpy as jnp
from jax import lax
from jax.experimental import pallas as pl
from jax.experimental.pallas import tpu as pltpu
from jax.sharding import PartitionSpec as P


def pick_kernel(count, tile, ids_ref, coef_ref, out_ref, sem):
    def begin(slot, carry):
        source = pl.ds(pl.multiple_of(ids_ref[slot] * tile, tile), tile)
        target = pl.ds(pl.multiple_of(slot * tile, tile), tile)
        pltpu.make_async_copy(coef_ref.at[:, source], out_ref.at[:, target], sem).start()
        return carry

    lax.fori_loop(0, count, begin, 0)
    pltpu.make_async_copy(coef_ref.at[:, pl.ds(0, count * tile)], out_ref, sem).wait()


def pick(coefficients, ids, tile):
    count = ids.shape[0]
    return pl.pallas_call(
        functools.partial(pick_kernel, count, tile),
        out_shape=jax.ShapeDtypeStruct((coefficients.shape[0], count * tile), coefficients.dtype),
        in_specs=[
            pl.BlockSpec(memory_space=pltpu.SMEM),
            pl.BlockSpec(memory_space=pl.ANY),
        ],
        out_specs=pl.BlockSpec(memory_space=pltpu.VMEM),
        scratch_shapes=[pltpu.SemaphoreType.DMA],
    )(ids, coefficients)


def per_device(rows, orbs, integrals, tile_ids, coefficients, metric):
    aux_local, local_rows, kept_width = integrals.shape
    orb_local, basis_width = coefficients.shape
    block_count, kept_count = tile_ids.shape
    tile_rows = local_rows // block_count
    orbitals = orb_local * orbs
    aux = aux_local * orbs
    window = local_rows * rows
    part = orbitals // (rows * orbs)
    picked = pick(coefficients, tile_ids.reshape(block_count * kept_count), tile_rows)
    col_piece = lax.all_gather(picked, "orb", axis=0, tiled=True)
    slabs = integrals.reshape(aux_local, block_count, tile_rows, kept_width)
    halves = [
        jnp.einsum(
            "pmk,jk->pjm",
            slabs[:, b],
            col_piece[:, b * kept_width : (b + 1) * kept_width],
            preferred_element_type=jnp.float32,
        ).astype(jnp.bfloat16)
        for b in range(block_count)
    ]
    halves = jnp.concatenate(halves, axis=2)
    outgoing = halves.reshape(aux_local, rows * orbs, part, local_rows).transpose(1, 0, 2, 3)
    by_part = lax.all_to_all(outgoing, ("row", "orb"), split_axis=0, concat_axis=0, tiled=True)
    by_part = by_part.reshape(rows, aux, part, local_rows)
    mixed = jnp.einsum(
        "pq,rpjm->rqjm", metric, by_part.astype(jnp.float32), precision=lax.Precision.HIGHEST
    ).astype(jnp.bfloat16)
    gram = jnp.einsum(
        "rqjm,sqjn->rmsn", by_part, mixed, preferred_element_type=jnp.float32
    ).astype(jnp.bfloat16)
    gram = gram.reshape(orbs, window // orbs, rows, local_rows).transpose(2, 0, 1, 3)
    gram = gram.reshape(rows * window, local_rows)
    share = lax.psum_scatter(gram, ("row", "orb"), scatter_dimension=0, tiled=True)
    columns = lax.all_gather(share, "orb", axis=0, tiled=True)
    return jnp.dot(coefficients[:, :window], columns, preferred_element_type=jnp.float32)


def solution(mesh):
    return jax.shard_map(
        functools.partial(per_device, mesh.shape["row"], mesh.shape["orb"]),
        mesh=mesh,
        in_specs=(P("orb", "row", None), P("row", None), P("orb", None), P()),
        out_specs=P("orb", "row"),
        check_vma=False,
    )
```

```python
import functools

import jax
import jax.numpy as jnp
from jax import lax
from jax.experimental import pallas as pl
from jax.experimental.pallas import tpu as pltpu
from jax.sharding import PartitionSpec as P


def pick_kernel(count, tile, ids_ref, coef_ref, out_ref, sem):
    def begin(slot, carry):
        source = pl.ds(pl.multiple_of(ids_ref[slot] * tile, tile), tile)
        target = pl.ds(pl.multiple_of(slot * tile, tile), tile)
        pltpu.make_async_copy(coef_ref.at[:, source], out_ref.at[:, target], sem).start()
        return carry

    lax.fori_loop(0, count, begin, 0)
    pltpu.make_async_copy(coef_ref.at[:, pl.ds(0, count * tile)], out_ref, sem).wait()


def pick(coefficients, ids, tile):
    count = ids.shape[0]
    return pl.pallas_call(
        functools.partial(pick_kernel, count, tile),
        out_shape=jax.ShapeDtypeStruct((coefficients.shape[0], count * tile), coefficients.dtype),
        in_specs=[
            pl.BlockSpec(memory_space=pltpu.SMEM),
            pl.BlockSpec(memory_space=pl.ANY),
        ],
        out_specs=pl.BlockSpec(memory_space=pltpu.VMEM),
        scratch_shapes=[pltpu.SemaphoreType.DMA],
    )(ids, coefficients)


MESH = pl.DeviceIdType.MESH
CORES = 2
SPLIT = 2


def greet(peers):
    barrier = pltpu.get_barrier_semaphore()
    for peer in peers:
        pl.semaphore_signal(barrier, inc=1, device_id=peer, device_id_type=MESH)
    pl.semaphore_wait(barrier, len(peers))


def remote(source, target, send, recv, device):
    return pltpu.make_async_remote_copy(
        src_ref=source,
        dst_ref=target,
        send_sem=send,
        recv_sem=recv,
        device_id=device,
        device_id_type=MESH,
    )


def gather_kernel(dims, ids_ref, coef_ref, ints_ref, kept_ref, other_ref, *scratch):
    rows, chips, orb_local, tile, count = dims
    quarter = orb_local // rows
    piece = quarter // SPLIT
    routes = [(d, s) for d in range(1, chips) for s in (1, -1)]
    scratch = list(scratch)
    raw = {}
    for route in range(len(routes)):
        for h in range(SPLIT):
            raw[route, h] = scratch.pop(0)
    staged = {}
    for route in range(len(routes)):
        for h in range(SPLIT):
            for t in range(rows):
                staged[route, h, t] = scratch.pop(0)
    own, own_kept, ids_v, ids_s, z_send, z_recv, p_send, p_recv, l_sem, i_send, i_recv = scratch
    row = lax.axis_index("row")
    orb = lax.axis_index("orb")
    chip = orb // CORES
    core = orb % CORES
    row_peers = [(lax.rem(row + t, rows), orb) for t in range(1, rows)]
    chip_peers = [(row, lax.rem(chip + d, chips) * CORES + core) for d in range(1, chips)]
    partner = (row, chip * CORES + 1 - core)
    greet(row_peers + chip_peers + [partner])

    def z_copy(route, h, device):
        rows_at = pl.ds(pl.multiple_of(row * quarter + h * piece, piece), piece)
        return remote(
            own.at[:, rows_at, :],
            raw[route, h],
            z_send.at[route, h],
            z_recv.at[route, h],
            device,
        )

    def towards(route):
        d, s = routes[route]
        there = chip + s * d
        return there, (there >= 0) & (there < chips)

    def origin(route):
        d, s = routes[route]
        there = chip - s * d
        return there, (there >= 0) & (there < chips)

    tiles = own.shape[0]

    def fetch(index, carry):
        at = pl.ds(pl.multiple_of(index * tile, tile), tile)
        pltpu.make_async_copy(coef_ref.at[:, at], own.at[index], l_sem.at[0]).start()
        return carry

    lax.fori_loop(0, tiles, fetch, 0)
    id_copies = []
    for t in range(1, rows):
        id_copies.append(
            remote(ids_ref, ids_v.at[t], i_send.at[t], i_recv.at[t], row_peers[t - 1])
        )
        id_copies[-1].start()

    def landed(index, carry):
        at = pl.ds(pl.multiple_of(index * tile, tile), tile)
        pltpu.make_async_copy(coef_ref.at[:, at], own.at[index], l_sem.at[0]).wait()
        return carry

    lax.fori_loop(0, tiles, landed, 0)
    for route in range(len(routes)):
        there, valid = towards(route)
        for h in range(SPLIT):

            @pl.when(valid)
            def _():
                z_copy(route, h, (row, there * CORES + core)).start()

    swap = remote(ints_ref, other_ref, i_send.at[0], i_recv.at[0], partner)
    swap.start()
    first = pltpu.make_async_copy(ids_ref, ids_s.at[0], l_sem.at[1])
    first.start()
    first.wait()
    for t in range(1, rows):
        id_copies[t - 1].wait()
        move = pltpu.make_async_copy(ids_v.at[t], ids_s.at[t], l_sem.at[1])
        move.start()
        move.wait()

    def take(source, target, t):
        step = 8

        def some(block, carry):
            for k in range(step):
                slot = block * step + k
                at = pl.multiple_of(slot * tile, tile)
                target[:, pl.ds(at, tile)] = source[ids_s[t, 0, slot]]
            return carry

        lax.fori_loop(0, count // step, some, 0)

    take(own, own_kept, 0)
    own_rows = pl.ds(pl.multiple_of(chip * orb_local, orb_local), orb_local)
    keep_own = pltpu.make_async_copy(own_kept, kept_ref.at[own_rows, :], l_sem.at[0])
    keep_own.start()

    def spread(route, h, t, from_row, from_chip, device):
        start = pl.multiple_of(from_chip * orb_local + from_row * quarter + h * piece, piece)
        return remote(
            staged[route, h, t],
            kept_ref.at[pl.ds(start, piece), :],
            p_send.at[route, h, t],
            p_recv.at[route, h, t],
            device,
        )

    def local(route, h, from_chip):
        start = pl.multiple_of(from_chip * orb_local + row * quarter + h * piece, piece)
        return pltpu.make_async_copy(
            staged[route, h, 0], kept_ref.at[pl.ds(start, piece), :], p_send.at[route, h, 0]
        )

    for d in range(1, chips):
        for h in range(SPLIT):
            for route in range(len(routes)):
                if routes[route][0] != d:
                    continue
                came, valid = origin(route)

                @pl.when(valid)
                def _():
                    z_copy(route, h, partner).wait_recv()
                    for t in range(1, rows):
                        take(raw[route, h], staged[route, h, t], t)
                        spread(route, h, t, row, came, row_peers[rows - t - 1]).start()
                    take(raw[route, h], staged[route, h, 0], 0)
                    local(route, h, came).start()

    for route in range(len(routes)):
        there, sent = towards(route)
        came, valid = origin(route)
        for h in range(SPLIT):

            @pl.when(sent)
            def _():
                z_copy(route, h, (row, there * CORES + core)).wait_send()

            @pl.when(valid)
            def _():
                local(route, h, came).wait()
                for t in range(1, rows):
                    spread(route, h, t, row, came, row_peers[rows - t - 1]).wait_send()
                    source_row = lax.rem(row + t, rows)
                    spread(route, h, t, source_row, came, row_peers[0]).wait_recv()

    keep_own.wait()
    swap.wait()


def gather(integrals, ids, coefficients, rows, orbs, tile, count):
    chips = orbs // CORES
    orb_local, basis = coefficients.shape
    piece = orb_local // rows // SPLIT
    routes = 2 * (chips - 1)
    dtype = coefficients.dtype
    scratch = [pltpu.VMEM((basis // tile, piece, tile), dtype) for _ in range(routes * SPLIT)]
    scratch += [pltpu.VMEM((piece, count * tile), dtype) for _ in range(routes * SPLIT * rows)]
    scratch += [
        pltpu.VMEM((basis // tile, orb_local, tile), dtype),
        pltpu.VMEM((orb_local, count * tile), dtype),
        pltpu.VMEM((rows, 1, ids.shape[1]), jnp.int32),
        pltpu.SMEM((rows, 1, ids.shape[1]), jnp.int32),
        pltpu.SemaphoreType.DMA((routes, SPLIT)),
        pltpu.SemaphoreType.DMA((routes, SPLIT)),
        pltpu.SemaphoreType.DMA((routes, SPLIT, rows)),
        pltpu.SemaphoreType.DMA((routes, SPLIT, rows)),
        pltpu.SemaphoreType.DMA((2,)),
        pltpu.SemaphoreType.DMA((rows,)),
        pltpu.SemaphoreType.DMA((rows,)),
    ]
    return pl.pallas_call(
        functools.partial(gather_kernel, (rows, chips, orb_local, tile, count)),
        out_shape=(
            jax.ShapeDtypeStruct((chips * orb_local, count * tile), dtype),
            jax.ShapeDtypeStruct(integrals.shape, integrals.dtype),
        ),
        in_specs=[pl.BlockSpec(memory_space=pltpu.VMEM)]
        + [pl.BlockSpec(memory_space=pl.ANY)] * 2,
        out_specs=(pl.BlockSpec(memory_space=pl.ANY), pl.BlockSpec(memory_space=pl.ANY)),
        scratch_shapes=scratch,
        compiler_params=pltpu.CompilerParams(
            collective_id=0, has_side_effects=True, vmem_limit_bytes=56 << 20
        ),
    )(ids, coefficients, integrals)


def exchange_kernel(rows, chips, in_ref, out_ref, send, recv, l_sem):
    row = lax.axis_index("row")
    orb = lax.axis_index("orb")
    core = orb % CORES
    me = row * chips + orb // CORES
    total = rows * chips

    def place(k):
        other = lax.rem(me + k, total)
        return other, (other // chips, lax.rem(other, chips) * CORES + core)

    greet([place(k)[1] for k in range(1, total)])
    stay = pltpu.make_async_copy(in_ref.at[me], out_ref.at[me], l_sem)
    stay.start()
    copies = []
    for k in range(1, total):
        other, device = place(k)
        copies.append(
            remote(in_ref.at[other], out_ref.at[me], send.at[k], recv.at[k], device)
        )
        copies[-1].start()
    stay.wait()
    for k in range(1, total):
        copies[k - 1].wait_send()
        other, device = place(total - k)
        remote(in_ref.at[me], out_ref.at[other], send.at[k], recv.at[k], device).wait_recv()


def exchange(outgoing, rows, chips):
    total = rows * chips
    return pl.pallas_call(
        functools.partial(exchange_kernel, rows, chips),
        out_shape=jax.ShapeDtypeStruct(outgoing.shape, outgoing.dtype),
        in_specs=[pl.BlockSpec(memory_space=pltpu.VMEM)],
        out_specs=pl.BlockSpec(memory_space=pltpu.VMEM),
        scratch_shapes=[
            pltpu.SemaphoreType.DMA((total,)),
            pltpu.SemaphoreType.DMA((total,)),
            pltpu.SemaphoreType.DMA,
        ],
        compiler_params=pltpu.CompilerParams(collective_id=1, has_side_effects=True),
    )(outgoing)


def finish_kernel(rows, orbs, gram_ref, coef_ref, out_ref, *scratch):
    (part1, sum1, part2, share, full, send1, recv1, send2, recv2, send3, recv3) = scratch
    row = lax.axis_index("row")
    orb = lax.axis_index("orb")
    height = share.shape[0]
    row_peers = [lax.rem(row + t, rows) for t in range(1, rows)]
    orb_peers = [lax.rem(orb + t, orbs) for t in range(1, orbs)]
    greet([(peer, orb) for peer in row_peers] + [(row, peer) for peer in orb_peers])
    copies = []
    for t, peer in enumerate(row_peers):
        copies.append(
            remote(gram_ref.at[peer], part1.at[t], send1.at[t], recv1.at[t], (peer, orb))
        )
        copies[-1].start()
    for copy in copies:
        copy.wait()
    total = gram_ref[row].astype(jnp.float32)
    for t in range(rows - 1):
        total = total + part1[t].astype(jnp.float32)
    sum1[...] = total.astype(sum1.dtype).reshape(sum1.shape)
    copies = []
    for t, peer in enumerate(orb_peers):
        copies.append(
            remote(sum1.at[peer], part2.at[t], send2.at[t], recv2.at[t], (row, peer))
        )
        copies[-1].start()
    for copy in copies:
        copy.wait()
    total = sum1[orb].astype(jnp.float32)
    for t in range(orbs - 1):
        total = total + part2[t].astype(jnp.float32)
    share[...] = total.astype(share.dtype)
    own_rows = pl.ds(pl.multiple_of(orb * height, height), height)
    copies = []
    for t, peer in enumerate(orb_peers):
        copies.append(
            remote(share, full.at[own_rows, :], send3.at[t], recv3.at[t], (row, peer))
        )
        copies[-1].start()
    full[own_rows, :] = share[...]
    for t in range(orbs - 1):
        copies[t].wait_send()
        source = lax.rem(orb + orbs - t - 1, orbs)
        rows_at = pl.ds(pl.multiple_of(source * height, height), height)
        remote(
            share, full.at[rows_at, :], send3.at[t], recv3.at[t], (row, orb_peers[0])
        ).wait_recv()
    out_ref[...] = jnp.dot(coef_ref[...], full[...], preferred_element_type=jnp.float32)


def finish(gram, coefs, rows, orbs):
    _, window, width = gram.shape
    height = window // orbs
    dtype = gram.dtype
    return pl.pallas_call(
        functools.partial(finish_kernel, rows, orbs),
        out_shape=jax.ShapeDtypeStruct((coefs.shape[0], width), jnp.float32),
        in_specs=[pl.BlockSpec(memory_space=pltpu.VMEM)] * 2,
        out_specs=pl.BlockSpec(memory_space=pltpu.VMEM),
        scratch_shapes=[
            pltpu.VMEM((rows - 1, window, width), dtype),
            pltpu.VMEM((orbs, height, width), dtype),
            pltpu.VMEM((orbs - 1, height, width), dtype),
            pltpu.VMEM((height, width), dtype),
            pltpu.VMEM((window, width), dtype),
            pltpu.SemaphoreType.DMA((rows,)),
            pltpu.SemaphoreType.DMA((rows,)),
            pltpu.SemaphoreType.DMA((orbs,)),
            pltpu.SemaphoreType.DMA((orbs,)),
            pltpu.SemaphoreType.DMA((orbs,)),
            pltpu.SemaphoreType.DMA((orbs,)),
        ],
        compiler_params=pltpu.CompilerParams(collective_id=2, has_side_effects=True),
    )(gram, coefs)


def per_device(rows, orbs, integrals, tile_ids, coefficients, metric):
    aux_local, local_rows, kept_width = integrals.shape
    orb_local, basis_width = coefficients.shape
    block_count, kept_count = tile_ids.shape
    if orb_local % (16 * SPLIT * rows) or orbs % CORES or (block_count * kept_count) % 8:
        return plain_device(rows, orbs, integrals, tile_ids, coefficients, metric)
    tile_rows = local_rows // block_count
    chips = orbs // CORES
    aux = aux_local * orbs
    window = local_rows * rows
    count = block_count * kept_count
    held = chips * orb_local
    part = held // (rows * chips)
    lanes = -(-count // 128) * 128
    ids = jnp.pad(tile_ids.reshape(1, count), ((0, 0), (0, lanes - count)))
    kept, other = gather(integrals, ids, coefficients, rows, orbs, tile_rows, count)
    halves = []
    for source in (integrals, other):
        slabs = source.reshape(aux_local, block_count, tile_rows, kept_width)
        blocks = [
            jnp.einsum(
                "pmk,jk->pjm",
                slabs[:, b],
                kept[:, b * kept_width : (b + 1) * kept_width],
                preferred_element_type=jnp.float32,
            ).astype(jnp.bfloat16)
            for b in range(block_count)
        ]
        halves.append(jnp.concatenate(blocks, axis=2))
    halves = jnp.concatenate(halves, axis=0)
    outgoing = halves.reshape(CORES * aux_local, rows * chips, part, local_rows)
    by_part = exchange(outgoing.transpose(1, 0, 2, 3), rows, chips)
    by_part = by_part.reshape(rows, aux, part, local_rows)
    core = lax.axis_index("orb") % CORES
    order = metric.reshape(chips, CORES, aux_local, chips, CORES, aux_local)
    order = jnp.where(core == 0, order, order[:, ::-1, :, :, ::-1, :]).reshape(aux, aux)
    mixed = jnp.einsum(
        "pq,rpjm->rqjm", order, by_part.astype(jnp.float32), precision=lax.Precision.HIGHEST
    ).astype(jnp.bfloat16)
    gram = jnp.einsum(
        "rqjm,sqjn->srmn", by_part, mixed, preferred_element_type=jnp.float32
    ).astype(jnp.bfloat16)
    gram = gram.reshape(rows, window, local_rows)
    return finish(gram, coefficients[:, :window], rows, orbs)


def plain_device(rows, orbs, integrals, tile_ids, coefficients, metric):
    aux_local, local_rows, kept_width = integrals.shape
    orb_local, basis_width = coefficients.shape
    block_count, kept_count = tile_ids.shape
    tile_rows = local_rows // block_count
    orbitals = orb_local * orbs
    aux = aux_local * orbs
    window = local_rows * rows
    part = orbitals // (rows * orbs)
    picked = pick(coefficients, tile_ids.reshape(block_count * kept_count), tile_rows)
    col_piece = lax.all_gather(picked, "orb", axis=0, tiled=True)
    slabs = integrals.reshape(aux_local, block_count, tile_rows, kept_width)
    halves = [
        jnp.einsum(
            "pmk,jk->pjm",
            slabs[:, b],
            col_piece[:, b * kept_width : (b + 1) * kept_width],
            preferred_element_type=jnp.float32,
        ).astype(jnp.bfloat16)
        for b in range(block_count)
    ]
    halves = jnp.concatenate(halves, axis=2)
    outgoing = halves.reshape(aux_local, rows * orbs, part, local_rows).transpose(1, 0, 2, 3)
    by_part = lax.all_to_all(outgoing, ("row", "orb"), split_axis=0, concat_axis=0, tiled=True)
    by_part = by_part.reshape(rows, aux, part, local_rows)
    mixed = jnp.einsum(
        "pq,rpjm->rqjm", metric, by_part.astype(jnp.float32), precision=lax.Precision.HIGHEST
    ).astype(jnp.bfloat16)
    gram = jnp.einsum(
        "rqjm,sqjn->rmsn", by_part, mixed, preferred_element_type=jnp.float32
    ).astype(jnp.bfloat16)
    gram = gram.reshape(orbs, window // orbs, rows, local_rows).transpose(2, 0, 1, 3)
    gram = gram.reshape(rows * window, local_rows)
    share = lax.psum_scatter(gram, ("row", "orb"), scatter_dimension=0, tiled=True)
    columns = lax.all_gather(share, "orb", axis=0, tiled=True)
    return jnp.dot(coefficients[:, :window], columns, preferred_element_type=jnp.float32)


def solution(mesh):
    return jax.shard_map(
        functools.partial(per_device, mesh.shape["row"], mesh.shape["orb"]),
        mesh=mesh,
        in_specs=(P("orb", "row", None), P("row", None), P("orb", None), P()),
        out_specs=P("orb", "row"),
        check_vma=False,
    )
```

```python
import functools

import jax
import jax.numpy as jnp
from jax import lax
from jax.experimental import pallas as pl
from jax.experimental.pallas import tpu as pltpu
from jax.sharding import PartitionSpec as P


def pick_kernel(count, tile, ids_ref, coef_ref, out_ref, sem):
    def begin(slot, carry):
        source = pl.ds(pl.multiple_of(ids_ref[slot] * tile, tile), tile)
        target = pl.ds(pl.multiple_of(slot * tile, tile), tile)
        pltpu.make_async_copy(coef_ref.at[:, source], out_ref.at[:, target], sem).start()
        return carry

    lax.fori_loop(0, count, begin, 0)
    pltpu.make_async_copy(coef_ref.at[:, pl.ds(0, count * tile)], out_ref, sem).wait()


def pick(coefficients, ids, tile):
    count = ids.shape[0]
    return pl.pallas_call(
        functools.partial(pick_kernel, count, tile),
        out_shape=jax.ShapeDtypeStruct((coefficients.shape[0], count * tile), coefficients.dtype),
        in_specs=[
            pl.BlockSpec(memory_space=pltpu.SMEM),
            pl.BlockSpec(memory_space=pl.ANY),
        ],
        out_specs=pl.BlockSpec(memory_space=pltpu.VMEM),
        scratch_shapes=[pltpu.SemaphoreType.DMA],
    )(ids, coefficients)


MESH = pl.DeviceIdType.MESH
CORES = 2
SPLIT = 2


def greet(peers):
    barrier = pltpu.get_barrier_semaphore()
    for peer in peers:
        pl.semaphore_signal(barrier, inc=1, device_id=peer, device_id_type=MESH)
    pl.semaphore_wait(barrier, len(peers))


def remote(source, target, send, recv, device):
    return pltpu.make_async_remote_copy(
        src_ref=source,
        dst_ref=target,
        send_sem=send,
        recv_sem=recv,
        device_id=device,
        device_id_type=MESH,
    )


def gather_kernel(dims, ids_ref, coef_ref, ints_ref, kept_ref, other_ref, *scratch):
    rows, chips, orb_local, tile, count = dims
    quarter = orb_local // rows
    piece = quarter // SPLIT
    routes = [(d, s) for d in range(1, chips) for s in (1, -1)]
    scratch = list(scratch)
    raw = {}
    for route in range(len(routes)):
        for h in range(SPLIT):
            raw[route, h] = scratch.pop(0)
    staged = {}
    for route in range(len(routes)):
        for h in range(SPLIT):
            for t in range(rows):
                staged[route, h, t] = scratch.pop(0)
    own, own_kept, ids_v, ids_s, z_send, z_recv, p_send, p_recv, l_sem, i_send, i_recv = scratch
    row = lax.axis_index("row")
    orb = lax.axis_index("orb")
    chip = orb // CORES
    core = orb % CORES
    row_peers = [(lax.rem(row + t, rows), orb) for t in range(1, rows)]
    chip_peers = [(row, lax.rem(chip + d, chips) * CORES + core) for d in range(1, chips)]
    partner = (row, chip * CORES + 1 - core)
    greet(row_peers + chip_peers + [partner])

    def z_copy(route, h, device):
        rows_at = pl.ds(pl.multiple_of(row * quarter + h * piece, piece), piece)
        return remote(
            own.at[:, rows_at, :] if routes[route][0] == 1 else raw[route - 2, h],
            raw[route, h],
            z_send.at[route, h],
            z_recv.at[route, h],
            device,
        )

    def towards(route):
        d, s = routes[route]
        there = chip + s
        start = chip - s * (d - 1)
        return there, (there >= 0) & (there < chips) & (start >= 0) & (start < chips)

    def origin(route):
        d, s = routes[route]
        there = chip - s * d
        return there, (there >= 0) & (there < chips)

    tiles = own.shape[0]

    def fetch(index, carry):
        at = pl.ds(pl.multiple_of(index * tile, tile), tile)
        pltpu.make_async_copy(coef_ref.at[:, at], own.at[index], l_sem.at[0]).start()
        return carry

    lax.fori_loop(0, tiles, fetch, 0)
    id_copies = []
    for t in range(1, rows):
        id_copies.append(
            remote(ids_ref, ids_v.at[t], i_send.at[t], i_recv.at[t], row_peers[t - 1])
        )
        id_copies[-1].start()

    def landed(index, carry):
        at = pl.ds(pl.multiple_of(index * tile, tile), tile)
        pltpu.make_async_copy(coef_ref.at[:, at], own.at[index], l_sem.at[0]).wait()
        return carry

    lax.fori_loop(0, tiles, landed, 0)
    for route in range(2):
        there, valid = towards(route)
        for h in range(SPLIT):

            @pl.when(valid)
            def _():
                z_copy(route, h, (row, there * CORES + core)).start()

    swap = remote(ints_ref, other_ref, i_send.at[0], i_recv.at[0], partner)
    swap.start()
    first = pltpu.make_async_copy(ids_ref, ids_s.at[0], l_sem.at[1])
    first.start()
    first.wait()
    for t in range(1, rows):
        id_copies[t - 1].wait()
        move = pltpu.make_async_copy(ids_v.at[t], ids_s.at[t], l_sem.at[1])
        move.start()
        move.wait()

    def take(source, target, t):
        step = 8

        def some(block, carry):
            for k in range(step):
                slot = block * step + k
                at = pl.multiple_of(slot * tile, tile)
                target[:, pl.ds(at, tile)] = source[ids_s[t, 0, slot]]
            return carry

        lax.fori_loop(0, count // step, some, 0)

    take(own, own_kept, 0)
    own_rows = pl.ds(pl.multiple_of(chip * orb_local, orb_local), orb_local)
    keep_own = pltpu.make_async_copy(own_kept, kept_ref.at[own_rows, :], l_sem.at[0])
    keep_own.start()

    def spread(route, h, t, from_row, from_chip, device):
        start = pl.multiple_of(from_chip * orb_local + from_row * quarter + h * piece, piece)
        return remote(
            staged[route, h, t],
            kept_ref.at[pl.ds(start, piece), :],
            p_send.at[route, h, t],
            p_recv.at[route, h, t],
            device,
        )

    def local(route, h, from_chip):
        start = pl.multiple_of(from_chip * orb_local + row * quarter + h * piece, piece)
        return pltpu.make_async_copy(
            staged[route, h, 0], kept_ref.at[pl.ds(start, piece), :], p_send.at[route, h, 0]
        )

    for d in range(1, chips):
        for h in range(SPLIT):
            for route in range(len(routes)):
                if routes[route][0] != d:
                    continue
                came, valid = origin(route)

                @pl.when(valid)
                def _():
                    z_copy(route, h, partner).wait_recv()
                    if d + 1 < chips:
                        there, onward = towards(route + 2)

                        @pl.when(onward)
                        def _():
                            z_copy(route + 2, h, (row, there * CORES + core)).start()

                    for t in range(1, rows):
                        take(raw[route, h], staged[route, h, t], t)
                        spread(route, h, t, row, came, row_peers[rows - t - 1]).start()
                    take(raw[route, h], staged[route, h, 0], 0)
                    local(route, h, came).start()

    for route in range(len(routes)):
        there, sent = towards(route)
        came, valid = origin(route)
        for h in range(SPLIT):

            @pl.when(sent)
            def _():
                z_copy(route, h, (row, there * CORES + core)).wait_send()

            @pl.when(valid)
            def _():
                local(route, h, came).wait()
                for t in range(1, rows):
                    spread(route, h, t, row, came, row_peers[rows - t - 1]).wait_send()
                    source_row = lax.rem(row + t, rows)
                    spread(route, h, t, source_row, came, row_peers[0]).wait_recv()

    keep_own.wait()
    swap.wait()


def gather(integrals, ids, coefficients, rows, orbs, tile, count):
    chips = orbs // CORES
    orb_local, basis = coefficients.shape
    piece = orb_local // rows // SPLIT
    routes = 2 * (chips - 1)
    dtype = coefficients.dtype
    scratch = [pltpu.VMEM((basis // tile, piece, tile), dtype) for _ in range(routes * SPLIT)]
    scratch += [pltpu.VMEM((piece, count * tile), dtype) for _ in range(routes * SPLIT * rows)]
    scratch += [
        pltpu.VMEM((basis // tile, orb_local, tile), dtype),
        pltpu.VMEM((orb_local, count * tile), dtype),
        pltpu.VMEM((rows, 1, ids.shape[1]), jnp.int32),
        pltpu.SMEM((rows, 1, ids.shape[1]), jnp.int32),
        pltpu.SemaphoreType.DMA((routes, SPLIT)),
        pltpu.SemaphoreType.DMA((routes, SPLIT)),
        pltpu.SemaphoreType.DMA((routes, SPLIT, rows)),
        pltpu.SemaphoreType.DMA((routes, SPLIT, rows)),
        pltpu.SemaphoreType.DMA((2,)),
        pltpu.SemaphoreType.DMA((rows,)),
        pltpu.SemaphoreType.DMA((rows,)),
    ]
    return pl.pallas_call(
        functools.partial(gather_kernel, (rows, chips, orb_local, tile, count)),
        out_shape=(
            jax.ShapeDtypeStruct((chips * orb_local, count * tile), dtype),
            jax.ShapeDtypeStruct(integrals.shape, integrals.dtype),
        ),
        in_specs=[pl.BlockSpec(memory_space=pltpu.VMEM)]
        + [pl.BlockSpec(memory_space=pl.ANY)] * 2,
        out_specs=(pl.BlockSpec(memory_space=pl.ANY), pl.BlockSpec(memory_space=pl.ANY)),
        scratch_shapes=scratch,
        compiler_params=pltpu.CompilerParams(
            collective_id=0, has_side_effects=True, vmem_limit_bytes=56 << 20
        ),
    )(ids, coefficients, integrals)


def exchange_kernel(rows, chips, in_ref, out_ref, send, recv, l_sem):
    row = lax.axis_index("row")
    orb = lax.axis_index("orb")
    core = orb % CORES
    me = row * chips + orb // CORES
    total = rows * chips

    def place(k):
        other = lax.rem(me + k, total)
        return other, (other // chips, lax.rem(other, chips) * CORES + core)

    greet([place(k)[1] for k in range(1, total)])
    stay = pltpu.make_async_copy(in_ref.at[me], out_ref.at[me], l_sem)
    stay.start()
    copies = []
    for k in range(1, total):
        other, device = place(k)
        copies.append(
            remote(in_ref.at[other], out_ref.at[me], send.at[k], recv.at[k], device)
        )
        copies[-1].start()
    stay.wait()
    for k in range(1, total):
        copies[k - 1].wait_send()
        other, device = place(total - k)
        remote(in_ref.at[me], out_ref.at[other], send.at[k], recv.at[k], device).wait_recv()


def exchange(outgoing, rows, chips):
    total = rows * chips
    return pl.pallas_call(
        functools.partial(exchange_kernel, rows, chips),
        out_shape=jax.ShapeDtypeStruct(outgoing.shape, outgoing.dtype),
        in_specs=[pl.BlockSpec(memory_space=pltpu.VMEM)],
        out_specs=pl.BlockSpec(memory_space=pltpu.VMEM),
        scratch_shapes=[
            pltpu.SemaphoreType.DMA((total,)),
            pltpu.SemaphoreType.DMA((total,)),
            pltpu.SemaphoreType.DMA,
        ],
        compiler_params=pltpu.CompilerParams(collective_id=1, has_side_effects=True),
    )(outgoing)


def finish_kernel(rows, chips, gram_ref, coef_ref, out_ref, *scratch):
    part0, sum0, part1, sum1, part2, share, full = scratch[:7]
    send0, recv0, send1, recv1, send2, recv2, send3, recv3 = scratch[7:]
    row = lax.axis_index("row")
    orb = lax.axis_index("orb")
    chip = orb // CORES
    core = orb % CORES
    height = share.shape[0]
    half = height * chips
    partner = (row, chip * CORES + 1 - core)
    row_peers = [lax.rem(row + t, rows) for t in range(1, rows)]
    chip_peers = [lax.rem(chip + t, chips) for t in range(1, chips)]
    greet(
        [partner]
        + [(peer, orb) for peer in row_peers]
        + [(row, peer * CORES + core) for peer in chip_peers]
    )
    order = row_peers + [row]
    first = []
    for t, peer in enumerate(order):
        first.append(
            remote(
                gram_ref.at[peer, 1 - core], part0.at[peer], send0.at[t], recv0.at[t], partner
            )
        )
        first[-1].start()
    second = []
    for t, peer in enumerate(order):
        first[t].wait_recv()
        total = gram_ref[peer, core].astype(jnp.float32) + part0[peer].astype(jnp.float32)
        sum0[peer] = total.astype(sum0.dtype)
        if t < rows - 1:
            second.append(
                remote(sum0.at[peer], part1.at[t], send1.at[t], recv1.at[t], (peer, orb))
            )
            second[-1].start()
    for copy in second:
        copy.wait_recv()
    total = sum0[row].astype(jnp.float32)
    for t in range(rows - 1):
        total = total + part1[t].astype(jnp.float32)
    sum1[...] = total.astype(sum1.dtype).reshape(sum1.shape)
    third = []
    for t, peer in enumerate(chip_peers):
        device = (row, peer * CORES + core)
        third.append(remote(sum1.at[peer], part2.at[t], send2.at[t], recv2.at[t], device))
        third[-1].start()
    for copy in third:
        copy.wait_recv()
    total = sum1[chip].astype(jnp.float32)
    for t in range(chips - 1):
        total = total + part2[t].astype(jnp.float32)
    share[...] = total.astype(share.dtype)

    def block(from_core, from_chip):
        start = pl.multiple_of(from_core * half + from_chip * height, height)
        return full.at[pl.ds(start, height), :]

    fourth = [
        remote(share, block(core, chip), send3.at[0, 0], recv3.at[0, 0], partner)
    ]
    for t, peer in enumerate(chip_peers):
        device = (row, peer * CORES + core)
        fourth.append(
            remote(share, block(core, chip), send3.at[0, t + 1], recv3.at[0, t + 1], device)
        )
    for copy in fourth:
        copy.start()
    full[pl.ds(pl.multiple_of(core * half + chip * height, height), height), :] = share[...]
    passed = []
    for t in range(1, chips):
        source = lax.rem(chip + chips - t, chips)
        remote(
            share, block(core, source), send3.at[0, t], recv3.at[0, t], partner
        ).wait_recv()
        passed.append(
            remote(
                block(core, source),
                block(core, source),
                send3.at[1, t],
                recv3.at[1, t],
                partner,
            )
        )
        passed[-1].start()
    mine = pl.ds(pl.multiple_of(core * half, half), half)
    theirs = pl.ds(pl.multiple_of((1 - core) * half, half), half)
    result = jnp.dot(coef_ref[:, mine], full[mine, :], preferred_element_type=jnp.float32)
    remote(share, block(1 - core, chip), send3.at[0, 0], recv3.at[0, 0], partner).wait_recv()
    for t in range(1, chips):
        source = lax.rem(chip + chips - t, chips)
        remote(
            block(core, source), block(1 - core, source), send3.at[1, t], recv3.at[1, t], partner
        ).wait_recv()
    out_ref[...] = result + jnp.dot(
        coef_ref[:, theirs], full[theirs, :], preferred_element_type=jnp.float32
    )
    for copy in first + second + third + fourth + passed:
        copy.wait_send()


def finish(gram, coefs, rows, chips):
    width = gram.shape[-1]
    half = gram.shape[2]
    height = half // chips
    dtype = gram.dtype
    return pl.pallas_call(
        functools.partial(finish_kernel, rows, chips),
        out_shape=jax.ShapeDtypeStruct((coefs.shape[0], width), jnp.float32),
        in_specs=[pl.BlockSpec(memory_space=pltpu.VMEM)] * 2,
        out_specs=pl.BlockSpec(memory_space=pltpu.VMEM),
        scratch_shapes=[
            pltpu.VMEM((rows, half, width), dtype),
            pltpu.VMEM((rows, half, width), dtype),
            pltpu.VMEM((rows - 1, half, width), dtype),
            pltpu.VMEM((chips, height, width), dtype),
            pltpu.VMEM((chips - 1, height, width), dtype),
            pltpu.VMEM((height, width), dtype),
            pltpu.VMEM((CORES * half, width), dtype),
            pltpu.SemaphoreType.DMA((rows,)),
            pltpu.SemaphoreType.DMA((rows,)),
            pltpu.SemaphoreType.DMA((rows,)),
            pltpu.SemaphoreType.DMA((rows,)),
            pltpu.SemaphoreType.DMA((chips,)),
            pltpu.SemaphoreType.DMA((chips,)),
            pltpu.SemaphoreType.DMA((CORES, chips)),
            pltpu.SemaphoreType.DMA((CORES, chips)),
        ],
        compiler_params=pltpu.CompilerParams(collective_id=2, has_side_effects=True),
    )(gram, coefs)


def per_device(rows, orbs, integrals, tile_ids, coefficients, metric):
    aux_local, local_rows, kept_width = integrals.shape
    orb_local, basis_width = coefficients.shape
    block_count, kept_count = tile_ids.shape
    if orb_local % (16 * SPLIT * rows) or orbs % CORES or (block_count * kept_count) % 8:
        return plain_device(rows, orbs, integrals, tile_ids, coefficients, metric)
    tile_rows = local_rows // block_count
    chips = orbs // CORES
    aux = aux_local * orbs
    window = local_rows * rows
    count = block_count * kept_count
    held = chips * orb_local
    part = held // (rows * chips)
    lanes = -(-count // 128) * 128
    ids = jnp.pad(tile_ids.reshape(1, count), ((0, 0), (0, lanes - count)))
    kept, other = gather(integrals, ids, coefficients, rows, orbs, tile_rows, count)
    halves = []
    for source in (integrals, other):
        slabs = source.reshape(aux_local, block_count, tile_rows, kept_width)
        blocks = [
            jnp.einsum(
                "pmk,jk->pjm",
                slabs[:, b],
                kept[:, b * kept_width : (b + 1) * kept_width],
                preferred_element_type=jnp.float32,
            ).astype(jnp.bfloat16)
            for b in range(block_count)
        ]
        halves.append(jnp.concatenate(blocks, axis=2))
    halves = jnp.concatenate(halves, axis=0)
    outgoing = halves.reshape(CORES * aux_local, rows * chips, part, local_rows)
    by_part = exchange(outgoing.transpose(1, 0, 2, 3), rows, chips)
    by_part = by_part.reshape(rows, aux, part, local_rows)
    core = lax.axis_index("orb") % CORES
    order = metric.reshape(chips, CORES, aux_local, chips, CORES, aux_local)
    order = jnp.where(core == 0, order, order[:, ::-1, :, :, ::-1, :]).reshape(aux, aux)
    mixed = jnp.einsum(
        "pq,rpjm->rqjm", order, by_part.astype(jnp.float32), precision=lax.Precision.HIGHEST
    ).astype(jnp.bfloat16)
    gram = jnp.einsum(
        "rqjm,sqjn->srmn", by_part, mixed, preferred_element_type=jnp.float32
    ).astype(jnp.bfloat16)
    gram = gram.reshape(rows, CORES, window // CORES, local_rows)
    return finish(gram, coefficients[:, :window], rows, chips)


def plain_device(rows, orbs, integrals, tile_ids, coefficients, metric):
    aux_local, local_rows, kept_width = integrals.shape
    orb_local, basis_width = coefficients.shape
    block_count, kept_count = tile_ids.shape
    tile_rows = local_rows // block_count
    orbitals = orb_local * orbs
    aux = aux_local * orbs
    window = local_rows * rows
    part = orbitals // (rows * orbs)
    picked = pick(coefficients, tile_ids.reshape(block_count * kept_count), tile_rows)
    col_piece = lax.all_gather(picked, "orb", axis=0, tiled=True)
    slabs = integrals.reshape(aux_local, block_count, tile_rows, kept_width)
    halves = [
        jnp.einsum(
            "pmk,jk->pjm",
            slabs[:, b],
            col_piece[:, b * kept_width : (b + 1) * kept_width],
            preferred_element_type=jnp.float32,
        ).astype(jnp.bfloat16)
        for b in range(block_count)
    ]
    halves = jnp.concatenate(halves, axis=2)
    outgoing = halves.reshape(aux_local, rows * orbs, part, local_rows).transpose(1, 0, 2, 3)
    by_part = lax.all_to_all(outgoing, ("row", "orb"), split_axis=0, concat_axis=0, tiled=True)
    by_part = by_part.reshape(rows, aux, part, local_rows)
    mixed = jnp.einsum(
        "pq,rpjm->rqjm", metric, by_part.astype(jnp.float32), precision=lax.Precision.HIGHEST
    ).astype(jnp.bfloat16)
    gram = jnp.einsum(
        "rqjm,sqjn->rmsn", by_part, mixed, preferred_element_type=jnp.float32
    ).astype(jnp.bfloat16)
    gram = gram.reshape(orbs, window // orbs, rows, local_rows).transpose(2, 0, 1, 3)
    gram = gram.reshape(rows * window, local_rows)
    share = lax.psum_scatter(gram, ("row", "orb"), scatter_dimension=0, tiled=True)
    columns = lax.all_gather(share, "orb", axis=0, tiled=True)
    return jnp.dot(coefficients[:, :window], columns, preferred_element_type=jnp.float32)


def solution(mesh):
    return jax.shard_map(
        functools.partial(per_device, mesh.shape["row"], mesh.shape["orb"]),
        mesh=mesh,
        in_specs=(P("orb", "row", None), P("row", None), P("orb", None), P()),
        out_specs=P("orb", "row"),
        check_vma=False,
    )
```

```python
import functools

import jax
import jax.numpy as jnp
from jax import lax
from jax.experimental import pallas as pl
from jax.experimental.pallas import tpu as pltpu
from jax.sharding import PartitionSpec as P


def pick_kernel(count, tile, ids_ref, coef_ref, out_ref, sem):
    def begin(slot, carry):
        source = pl.ds(pl.multiple_of(ids_ref[slot] * tile, tile), tile)
        target = pl.ds(pl.multiple_of(slot * tile, tile), tile)
        pltpu.make_async_copy(coef_ref.at[:, source], out_ref.at[:, target], sem).start()
        return carry

    lax.fori_loop(0, count, begin, 0)
    pltpu.make_async_copy(coef_ref.at[:, pl.ds(0, count * tile)], out_ref, sem).wait()


def pick(coefficients, ids, tile):
    count = ids.shape[0]
    return pl.pallas_call(
        functools.partial(pick_kernel, count, tile),
        out_shape=jax.ShapeDtypeStruct((coefficients.shape[0], count * tile), coefficients.dtype),
        in_specs=[
            pl.BlockSpec(memory_space=pltpu.SMEM),
            pl.BlockSpec(memory_space=pl.ANY),
        ],
        out_specs=pl.BlockSpec(memory_space=pltpu.VMEM),
        scratch_shapes=[pltpu.SemaphoreType.DMA],
    )(ids, coefficients)


MESH = pl.DeviceIdType.MESH
CORES = 2
SPLIT = 2


def greet(peers):
    barrier = pltpu.get_barrier_semaphore()
    for peer in peers:
        pl.semaphore_signal(barrier, inc=1, device_id=peer, device_id_type=MESH)
    pl.semaphore_wait(barrier, len(peers))


def remote(source, target, send, recv, device):
    return pltpu.make_async_remote_copy(
        src_ref=source,
        dst_ref=target,
        send_sem=send,
        recv_sem=recv,
        device_id=device,
        device_id_type=MESH,
    )


def halves_kernel(dims, ids_ref, coef_ref, ints_ref, out_ref, *scratch):
    rows, chips, orb_local, tile, count, aux_local, blocks, part = dims
    quarter = orb_local // rows
    piece = quarter // SPLIT
    routes = [(d, s) for d in range(1, chips) for s in (1, -1)]
    scratch = list(scratch)
    raw = {}
    for route in range(len(routes)):
        for h in range(SPLIT):
            raw[route, h] = scratch.pop(0)
    own, kept, staged, both, ready, ids_v, ids_s = scratch[:7]
    z_send, z_recv, p_send, p_recv, l_sem, i_send, i_recv, x_send, x_recv = scratch[7:]
    width = count * tile // blocks
    total = rows * chips
    row = lax.axis_index("row")
    orb = lax.axis_index("orb")
    chip = orb // CORES
    core = orb % CORES
    row_peers = [(lax.rem(row + t, rows), orb) for t in range(1, rows)]
    partner = (row, chip * CORES + 1 - core)
    me = row * chips + chip

    def place(k):
        other = lax.rem(me + k, total)
        return other, (other // chips, lax.rem(other, chips) * CORES + core)

    greet([place(k)[1] for k in range(1, total)] + [partner])

    def z_copy(route, h, device):
        rows_at = pl.ds(pl.multiple_of(row * quarter + h * piece, piece), piece)
        return remote(
            own.at[:, rows_at, :] if routes[route][0] == 1 else raw[route - 2, h],
            raw[route, h],
            z_send.at[route, h],
            z_recv.at[route, h],
            device,
        )

    def towards(route):
        d, s = routes[route]
        there = chip + s
        start = chip - s * (d - 1)
        return there, (there >= 0) & (there < chips) & (start >= 0) & (start < chips)

    def origin(route):
        d, s = routes[route]
        there = chip - s * d
        return there, (there >= 0) & (there < chips)

    tiles = own.shape[0]

    def fetch(index, carry):
        at = pl.ds(pl.multiple_of(index * tile, tile), tile)
        pltpu.make_async_copy(coef_ref.at[:, at], own.at[index], l_sem.at[0]).start()
        return carry

    lax.fori_loop(0, tiles, fetch, 0)
    id_copies = []
    for t in range(1, rows):
        id_copies.append(
            remote(ids_ref, ids_v.at[t], i_send.at[t], i_recv.at[t], row_peers[t - 1])
        )
        id_copies[-1].start()

    def landed(index, carry):
        at = pl.ds(pl.multiple_of(index * tile, tile), tile)
        pltpu.make_async_copy(coef_ref.at[:, at], own.at[index], l_sem.at[0]).wait()
        return carry

    lax.fori_loop(0, tiles, landed, 0)
    for route in range(2):
        there, valid = towards(route)
        for h in range(SPLIT):

            @pl.when(valid)
            def _():
                z_copy(route, h, (row, there * CORES + core)).start()

    swap = remote(ints_ref, both.at[1], i_send.at[0], i_recv.at[0], partner)
    swap.start()
    bring = pltpu.make_async_copy(ints_ref, both.at[0], l_sem.at[2])
    bring.start()
    first = pltpu.make_async_copy(ids_ref, ids_s.at[0], l_sem.at[1])
    first.start()
    first.wait()
    for t in range(1, rows):
        id_copies[t - 1].wait()
        move = pltpu.make_async_copy(ids_v.at[t], ids_s.at[t], l_sem.at[1])
        move.start()
        move.wait()

    def take(source, target, t):
        step = 8

        def some(block, carry):
            for k in range(step):
                slot = block * step + k
                at = pl.multiple_of(slot * tile, tile)
                target[:, pl.ds(at, tile)] = source[ids_s[t, 0, slot]]
            return carry

        lax.fori_loop(0, count // step, some, 0)

    def band(from_row, h):
        return pl.ds(pl.multiple_of(from_row * quarter + h * piece, piece), piece)

    def spread(from_row, came, h, t, device):
        k = lax.rem(came + chips - chip, chips) - 1
        return remote(
            staged.at[k, h, t - 1],
            kept.at[came, band(from_row, h), :],
            p_send.at[k, h, t],
            p_recv.at[k, h, t],
            device,
        )

    def handout(came, k):
        other, device = place(k)
        return remote(
            ready.at[came, other],
            out_ref.at[me, :, came],
            x_send.at[came, k],
            x_recv.at[came, k],
            device,
        )

    def keep(came):
        return pltpu.make_async_copy(
            ready.at[came, me], out_ref.at[me, :, came], x_send.at[came, 0]
        )

    def product(came):
        def one(step, carry):
            side = step // blocks
            block = step - side * blocks
            lhs = kept[came, :, pl.ds(pl.multiple_of(block * width, width), width)]
            at = pl.ds(pl.multiple_of(block * tile, tile), tile)
            rhs = both[side, :, at, :].reshape(aux_local * tile, width)
            result = lax.dot_general(
                lhs, rhs, (((1,), (1,)), ((), ())), preferred_element_type=jnp.float32
            )
            for p in range(aux_local):
                value = result[:, p * tile : (p + 1) * tile].astype(ready.dtype)
                ready[came, :, side * aux_local + p, :, at] = value.reshape(total, part, tile)
            return carry

        lax.fori_loop(0, CORES * blocks, one, 0)
        for k in range(1, total):
            handout(came, k).start()
        keep(came).start()

    take(own, kept.at[chip], 0)

    def pass_on(d):
        for h in range(SPLIT):
            for route in range(len(routes)):
                if routes[route][0] != d:
                    continue
                came, valid = origin(route)

                @pl.when(valid)
                def _():
                    z_copy(route, h, partner).wait_recv()
                    if d + 1 < chips:
                        there, onward = towards(route + 2)

                        @pl.when(onward)
                        def _():
                            z_copy(route + 2, h, (row, there * CORES + core)).start()

                    k = lax.rem(came + chips - chip, chips) - 1
                    for t in range(1, rows):
                        take(raw[route, h], staged.at[k, h, t - 1], t)
                        spread(row, came, h, t, row_peers[rows - t - 1]).start()
                    take(raw[route, h], kept.at[came, band(row, h), :], 0)

    def multiply(d):
        for route in range(len(routes)):
            if routes[route][0] != d:
                continue
            came, valid = origin(route)

            @pl.when(valid)
            def _():
                for h in range(SPLIT):
                    for t in range(1, rows):
                        source_row = lax.rem(row + t, rows)
                        spread(source_row, came, h, t, row_peers[0]).wait_recv()
                product(came)

    for d in range(1, chips):
        pass_on(d)
        if d == 1:
            bring.wait()
            swap.wait()
            product(chip)
        else:
            multiply(d - 1)
    multiply(chips - 1)

    for route in range(len(routes)):
        there, sent = towards(route)
        came, valid = origin(route)
        for h in range(SPLIT):

            @pl.when(sent)
            def _():
                z_copy(route, h, (row, there * CORES + core)).wait_send()

            @pl.when(valid)
            def _():
                for t in range(1, rows):
                    spread(row, came, h, t, row_peers[rows - t - 1]).wait_send()

    for came in range(chips):
        keep(came).wait()
        for k in range(1, total):
            handout(came, k).wait_send()
            other, device = place(total - k)
            remote(
                ready.at[came, me],
                out_ref.at[other, :, came],
                x_send.at[came, k],
                x_recv.at[came, k],
                device,
            ).wait_recv()


def halves_by_part(integrals, ids, coefficients, rows, orbs, blocks, count):
    chips = orbs // CORES
    orb_local, basis = coefficients.shape
    aux_local, local_rows, _ = integrals.shape
    tile = local_rows // blocks
    total = rows * chips
    part = orb_local // total
    piece = orb_local // rows // SPLIT
    routes = 2 * (chips - 1)
    dtype = coefficients.dtype
    scratch = [
        pltpu.VMEM((basis // tile, piece, tile), dtype) for _ in range(routes * SPLIT)
    ]
    scratch += [
        pltpu.VMEM((basis // tile, orb_local, tile), dtype),
        pltpu.VMEM((chips, orb_local, count * tile), dtype),
        pltpu.VMEM((chips - 1, SPLIT, rows - 1, piece, count * tile), dtype),
        pltpu.VMEM((CORES,) + integrals.shape, dtype),
        pltpu.VMEM((chips, total, CORES * aux_local, part, local_rows), dtype),
        pltpu.VMEM((rows, 1, ids.shape[1]), jnp.int32),
        pltpu.SMEM((rows, 1, ids.shape[1]), jnp.int32),
        pltpu.SemaphoreType.DMA((routes, SPLIT)),
        pltpu.SemaphoreType.DMA((routes, SPLIT)),
        pltpu.SemaphoreType.DMA((chips - 1, SPLIT, rows)),
        pltpu.SemaphoreType.DMA((chips - 1, SPLIT, rows)),
        pltpu.SemaphoreType.DMA((3,)),
        pltpu.SemaphoreType.DMA((rows,)),
        pltpu.SemaphoreType.DMA((rows,)),
        pltpu.SemaphoreType.DMA((chips, total)),
        pltpu.SemaphoreType.DMA((chips, total)),
    ]
    dims = (rows, chips, orb_local, tile, count, aux_local, blocks, part)
    return pl.pallas_call(
        functools.partial(halves_kernel, dims),
        out_shape=jax.ShapeDtypeStruct(
            (total, CORES * aux_local, chips, part, local_rows), dtype
        ),
        in_specs=[pl.BlockSpec(memory_space=pltpu.VMEM)]
        + [pl.BlockSpec(memory_space=pl.ANY)] * 2,
        out_specs=pl.BlockSpec(memory_space=pl.ANY),
        scratch_shapes=scratch,
        compiler_params=pltpu.CompilerParams(
            collective_id=0, has_side_effects=True, vmem_limit_bytes=60 << 20
        ),
    )(ids, coefficients, integrals)


def finish_kernel(rows, chips, gram_ref, coef_ref, out_ref, *scratch):
    part0, sum0, part1, sum1, part2, share, full = scratch[:7]
    send0, recv0, send1, recv1, send2, recv2, send3, recv3 = scratch[7:]
    row = lax.axis_index("row")
    orb = lax.axis_index("orb")
    chip = orb // CORES
    core = orb % CORES
    height = share.shape[0]
    half = height * chips
    partner = (row, chip * CORES + 1 - core)
    row_peers = [lax.rem(row + t, rows) for t in range(1, rows)]
    chip_peers = [lax.rem(chip + t, chips) for t in range(1, chips)]
    greet(
        [partner]
        + [(peer, orb) for peer in row_peers]
        + [(row, peer * CORES + core) for peer in chip_peers]
    )
    order = row_peers + [row]
    first = []
    for t, peer in enumerate(order):
        first.append(
            remote(
                gram_ref.at[peer, 1 - core], part0.at[peer], send0.at[t], recv0.at[t], partner
            )
        )
        first[-1].start()
    second = []
    for t, peer in enumerate(order):
        first[t].wait_recv()
        total = gram_ref[peer, core].astype(jnp.float32) + part0[peer].astype(jnp.float32)
        sum0[peer] = total.astype(sum0.dtype)
        if t < rows - 1:
            second.append(
                remote(sum0.at[peer], part1.at[t], send1.at[t], recv1.at[t], (peer, orb))
            )
            second[-1].start()
    for copy in second:
        copy.wait_recv()
    total = sum0[row].astype(jnp.float32)
    for t in range(rows - 1):
        total = total + part1[t].astype(jnp.float32)
    sum1[...] = total.astype(sum1.dtype).reshape(sum1.shape)
    third = []
    for t, peer in enumerate(chip_peers):
        device = (row, peer * CORES + core)
        third.append(remote(sum1.at[peer], part2.at[t], send2.at[t], recv2.at[t], device))
        third[-1].start()
    for copy in third:
        copy.wait_recv()
    total = sum1[chip].astype(jnp.float32)
    for t in range(chips - 1):
        total = total + part2[t].astype(jnp.float32)
    share[...] = total.astype(share.dtype)

    def block(from_core, from_chip):
        start = pl.multiple_of(from_core * half + from_chip * height, height)
        return full.at[pl.ds(start, height), :]

    fourth = [
        remote(share, block(core, chip), send3.at[0, 0], recv3.at[0, 0], partner)
    ]
    for t, peer in enumerate(chip_peers):
        device = (row, peer * CORES + core)
        fourth.append(
            remote(share, block(core, chip), send3.at[0, t + 1], recv3.at[0, t + 1], device)
        )
    for copy in fourth:
        copy.start()
    full[pl.ds(pl.multiple_of(core * half + chip * height, height), height), :] = share[...]
    passed = []
    for t in range(1, chips):
        source = lax.rem(chip + chips - t, chips)
        remote(
            share, block(core, source), send3.at[0, t], recv3.at[0, t], partner
        ).wait_recv()
        passed.append(
            remote(
                block(core, source),
                block(core, source),
                send3.at[1, t],
                recv3.at[1, t],
                partner,
            )
        )
        passed[-1].start()
    mine = pl.ds(pl.multiple_of(core * half, half), half)
    theirs = pl.ds(pl.multiple_of((1 - core) * half, half), half)
    result = jnp.dot(coef_ref[:, mine], full[mine, :], preferred_element_type=jnp.float32)
    remote(share, block(1 - core, chip), send3.at[0, 0], recv3.at[0, 0], partner).wait_recv()
    for t in range(1, chips):
        source = lax.rem(chip + chips - t, chips)
        remote(
            block(core, source), block(1 - core, source), send3.at[1, t], recv3.at[1, t], partner
        ).wait_recv()
    out_ref[...] = result + jnp.dot(
        coef_ref[:, theirs], full[theirs, :], preferred_element_type=jnp.float32
    )
    for copy in first + second + third + fourth + passed:
        copy.wait_send()


def finish(gram, coefs, rows, chips):
    width = gram.shape[-1]
    half = gram.shape[2]
    height = half // chips
    dtype = gram.dtype
    return pl.pallas_call(
        functools.partial(finish_kernel, rows, chips),
        out_shape=jax.ShapeDtypeStruct((coefs.shape[0], width), jnp.float32),
        in_specs=[pl.BlockSpec(memory_space=pltpu.VMEM)] * 2,
        out_specs=pl.BlockSpec(memory_space=pltpu.VMEM),
        scratch_shapes=[
            pltpu.VMEM((rows, half, width), dtype),
            pltpu.VMEM((rows, half, width), dtype),
            pltpu.VMEM((rows - 1, half, width), dtype),
            pltpu.VMEM((chips, height, width), dtype),
            pltpu.VMEM((chips - 1, height, width), dtype),
            pltpu.VMEM((height, width), dtype),
            pltpu.VMEM((CORES * half, width), dtype),
            pltpu.SemaphoreType.DMA((rows,)),
            pltpu.SemaphoreType.DMA((rows,)),
            pltpu.SemaphoreType.DMA((rows,)),
            pltpu.SemaphoreType.DMA((rows,)),
            pltpu.SemaphoreType.DMA((chips,)),
            pltpu.SemaphoreType.DMA((chips,)),
            pltpu.SemaphoreType.DMA((CORES, chips)),
            pltpu.SemaphoreType.DMA((CORES, chips)),
        ],
        compiler_params=pltpu.CompilerParams(collective_id=2, has_side_effects=True),
    )(gram, coefs)


def per_device(rows, orbs, integrals, tile_ids, coefficients, metric):
    aux_local, local_rows, kept_width = integrals.shape
    orb_local, basis_width = coefficients.shape
    block_count, kept_count = tile_ids.shape
    if orb_local % (16 * SPLIT * rows) or orb_local * CORES % (8 * rows * orbs) or block_count * kept_count % 8:
        return plain_device(rows, orbs, integrals, tile_ids, coefficients, metric)
    chips = orbs // CORES
    aux = aux_local * orbs
    window = local_rows * rows
    count = block_count * kept_count
    held = chips * orb_local
    part = held // (rows * chips)
    lanes = -(-count // 128) * 128
    ids = jnp.pad(tile_ids.reshape(1, count), ((0, 0), (0, lanes - count)))
    by_part = halves_by_part(integrals, ids, coefficients, rows, orbs, block_count, count)
    by_part = by_part.reshape(rows, aux, part, local_rows)
    core = lax.axis_index("orb") % CORES
    order = metric.reshape(chips, CORES, aux_local, chips, CORES, aux_local)
    order = jnp.where(core == 0, order, order[:, ::-1, :, :, ::-1, :]).reshape(aux, aux)
    mixed = jnp.einsum(
        "pq,rpjm->rqjm", order, by_part.astype(jnp.float32), precision=lax.Precision.HIGHEST
    ).astype(jnp.bfloat16)
    gram = jnp.einsum(
        "rqjm,sqjn->srmn", by_part, mixed, preferred_element_type=jnp.float32
    ).astype(jnp.bfloat16)
    gram = gram.reshape(rows, CORES, window // CORES, local_rows)
    return finish(gram, coefficients[:, :window], rows, chips)


def plain_device(rows, orbs, integrals, tile_ids, coefficients, metric):
    aux_local, local_rows, kept_width = integrals.shape
    orb_local, basis_width = coefficients.shape
    block_count, kept_count = tile_ids.shape
    tile_rows = local_rows // block_count
    orbitals = orb_local * orbs
    aux = aux_local * orbs
    window = local_rows * rows
    part = orbitals // (rows * orbs)
    picked = pick(coefficients, tile_ids.reshape(block_count * kept_count), tile_rows)
    col_piece = lax.all_gather(picked, "orb", axis=0, tiled=True)
    slabs = integrals.reshape(aux_local, block_count, tile_rows, kept_width)
    halves = [
        jnp.einsum(
            "pmk,jk->pjm",
            slabs[:, b],
            col_piece[:, b * kept_width : (b + 1) * kept_width],
            preferred_element_type=jnp.float32,
        ).astype(jnp.bfloat16)
        for b in range(block_count)
    ]
    halves = jnp.concatenate(halves, axis=2)
    outgoing = halves.reshape(aux_local, rows * orbs, part, local_rows).transpose(1, 0, 2, 3)
    by_part = lax.all_to_all(outgoing, ("row", "orb"), split_axis=0, concat_axis=0, tiled=True)
    by_part = by_part.reshape(rows, aux, part, local_rows)
    mixed = jnp.einsum(
        "pq,rpjm->rqjm", metric, by_part.astype(jnp.float32), precision=lax.Precision.HIGHEST
    ).astype(jnp.bfloat16)
    gram = jnp.einsum(
        "rqjm,sqjn->rmsn", by_part, mixed, preferred_element_type=jnp.float32
    ).astype(jnp.bfloat16)
    gram = gram.reshape(orbs, window // orbs, rows, local_rows).transpose(2, 0, 1, 3)
    gram = gram.reshape(rows * window, local_rows)
    share = lax.psum_scatter(gram, ("row", "orb"), scatter_dimension=0, tiled=True)
    columns = lax.all_gather(share, "orb", axis=0, tiled=True)
    return jnp.dot(coefficients[:, :window], columns, preferred_element_type=jnp.float32)


def solution(mesh):
    return jax.shard_map(
        functools.partial(per_device, mesh.shape["row"], mesh.shape["orb"]),
        mesh=mesh,
        in_specs=(P("orb", "row", None), P("row", None), P("orb", None), P()),
        out_specs=P("orb", "row"),
        check_vma=False,
    )
```

```python
import functools

import jax
import jax.numpy as jnp
from jax import lax
from jax.experimental import pallas as pl
from jax.experimental.pallas import tpu as pltpu
from jax.sharding import PartitionSpec as P


def pick_kernel(count, tile, ids_ref, coef_ref, out_ref, sem):
    def begin(slot, carry):
        source = pl.ds(pl.multiple_of(ids_ref[slot] * tile, tile), tile)
        target = pl.ds(pl.multiple_of(slot * tile, tile), tile)
        pltpu.make_async_copy(coef_ref.at[:, source], out_ref.at[:, target], sem).start()
        return carry

    lax.fori_loop(0, count, begin, 0)
    pltpu.make_async_copy(coef_ref.at[:, pl.ds(0, count * tile)], out_ref, sem).wait()


def pick(coefficients, ids, tile):
    count = ids.shape[0]
    return pl.pallas_call(
        functools.partial(pick_kernel, count, tile),
        out_shape=jax.ShapeDtypeStruct((coefficients.shape[0], count * tile), coefficients.dtype),
        in_specs=[
            pl.BlockSpec(memory_space=pltpu.SMEM),
            pl.BlockSpec(memory_space=pl.ANY),
        ],
        out_specs=pl.BlockSpec(memory_space=pltpu.VMEM),
        scratch_shapes=[pltpu.SemaphoreType.DMA],
    )(ids, coefficients)


MESH = pl.DeviceIdType.MESH
CORES = 2
SPLIT = 2


def greet(peers):
    barrier = pltpu.get_barrier_semaphore()
    for peer in peers:
        pl.semaphore_signal(barrier, inc=1, device_id=peer, device_id_type=MESH)
    pl.semaphore_wait(barrier, len(peers))


def remote(source, target, send, recv, device):
    return pltpu.make_async_remote_copy(
        src_ref=source,
        dst_ref=target,
        send_sem=send,
        recv_sem=recv,
        device_id=device,
        device_id_type=MESH,
    )


def halves_kernel(dims, ids_ref, coef_ref, ints_ref, out_ref, *scratch):
    rows, chips, orb_local, tile, count, aux_local, blocks, part = dims
    quarter = orb_local // rows
    piece = quarter // SPLIT
    routes = [(d, s) for d in range(1, chips) for s in (1, -1)]
    scratch = list(scratch)
    raw = {}
    for route in range(len(routes)):
        for h in range(SPLIT):
            raw[route, h] = scratch.pop(0)
    own, first_rows, kept, staged, both, ready, ids_v, ids_s = scratch[:8]
    z_send, z_recv, p_send, p_recv, l_sem, i_send, i_recv, x_send, x_recv = scratch[8:]
    width = count * tile // blocks
    total = rows * chips
    row = lax.axis_index("row")
    orb = lax.axis_index("orb")
    chip = orb // CORES
    core = orb % CORES
    row_peers = [(lax.rem(row + t, rows), orb) for t in range(1, rows)]
    partner = (row, chip * CORES + 1 - core)
    me = row * chips + chip

    def place(k):
        other = lax.rem(me + k, total)
        return other, (other // chips, lax.rem(other, chips) * CORES + core)

    greet([place(k)[1] for k in range(1, total)] + [partner])

    def z_copy(route, h, device):
        return remote(
            first_rows.at[:, pl.ds(h * piece, piece), :] if routes[route][0] == 1 else raw[route - 2, h],
            raw[route, h],
            z_send.at[route, h],
            z_recv.at[route, h],
            device,
        )

    def towards(route):
        d, s = routes[route]
        there = chip + s
        start = chip - s * (d - 1)
        return there, (there >= 0) & (there < chips) & (start >= 0) & (start < chips)

    def origin(route):
        d, s = routes[route]
        there = chip - s * d
        return there, (there >= 0) & (there < chips)

    tiles = own.shape[0]

    def tile_copy(index, source_rows, target, sem):
        at = pl.ds(pl.multiple_of(index * tile, tile), tile)
        return pltpu.make_async_copy(coef_ref.at[source_rows, at], target.at[index], sem)

    def every(source_rows, target, sem, act):
        def some(index, carry):
            act(tile_copy(index, source_rows, target, sem))
            return carry

        lax.fori_loop(0, tiles, some, 0)

    quarter_rows = pl.ds(pl.multiple_of(row * quarter, quarter), quarter)
    all_rows = pl.ds(0, orb_local)
    every(quarter_rows, first_rows, l_sem.at[3], lambda copy: copy.start())
    id_copies = []
    for t in range(1, rows):
        id_copies.append(
            remote(ids_ref, ids_v.at[t], i_send.at[t], i_recv.at[t], row_peers[t - 1])
        )
        id_copies[-1].start()

    every(quarter_rows, first_rows, l_sem.at[3], lambda copy: copy.wait())
    for route in range(2):
        there, valid = towards(route)
        for h in range(SPLIT):

            @pl.when(valid)
            def _():
                z_copy(route, h, (row, there * CORES + core)).start()

    every(all_rows, own, l_sem.at[0], lambda copy: copy.start())
    swap = remote(ints_ref, both.at[1], i_send.at[0], i_recv.at[0], partner)
    swap.start()
    bring = pltpu.make_async_copy(ints_ref, both.at[0], l_sem.at[2])
    bring.start()
    first = pltpu.make_async_copy(ids_ref, ids_s.at[0], l_sem.at[1])
    first.start()
    first.wait()
    for t in range(1, rows):
        id_copies[t - 1].wait()
        move = pltpu.make_async_copy(ids_v.at[t], ids_s.at[t], l_sem.at[1])
        move.start()
        move.wait()

    def take(source, target, t):
        step = 8

        def some(block, carry):
            for k in range(step):
                slot = block * step + k
                at = pl.multiple_of(slot * tile, tile)
                target[:, pl.ds(at, tile)] = source[ids_s[t, 0, slot]]
            return carry

        lax.fori_loop(0, count // step, some, 0)

    def band(from_row, h):
        return pl.ds(pl.multiple_of(from_row * quarter + h * piece, piece), piece)

    def spread(from_row, came, h, t, device):
        k = lax.rem(came + chips - chip, chips) - 1
        return remote(
            staged.at[k, h, t - 1],
            kept.at[came, band(from_row, h), :],
            p_send.at[k, h, t],
            p_recv.at[k, h, t],
            device,
        )

    def handout(came, k):
        other, device = place(k)
        return remote(
            ready.at[came, other],
            out_ref.at[me, :, came],
            x_send.at[came, k],
            x_recv.at[came, k],
            device,
        )

    def keep(came):
        return pltpu.make_async_copy(
            ready.at[came, me], out_ref.at[me, :, came], x_send.at[came, 0]
        )

    def product(came):
        def one(step, carry):
            side = step // blocks
            block = step - side * blocks
            lhs = kept[came, :, pl.ds(pl.multiple_of(block * width, width), width)]
            at = pl.ds(pl.multiple_of(block * tile, tile), tile)
            rhs = both[side, :, at, :].reshape(aux_local * tile, width)
            result = lax.dot_general(
                lhs, rhs, (((1,), (1,)), ((), ())), preferred_element_type=jnp.float32
            )
            for p in range(aux_local):
                value = result[:, p * tile : (p + 1) * tile].astype(ready.dtype)
                ready[came, :, side * aux_local + p, :, at] = value.reshape(total, part, tile)
            return carry

        lax.fori_loop(0, CORES * blocks, one, 0)
        for k in range(1, total):
            handout(came, k).start()
        keep(came).start()

    every(all_rows, own, l_sem.at[0], lambda copy: copy.wait())
    take(own, kept.at[chip], 0)

    def pass_on(d):
        for h in range(SPLIT):
            for route in range(len(routes)):
                if routes[route][0] != d:
                    continue
                came, valid = origin(route)

                @pl.when(valid)
                def _():
                    z_copy(route, h, partner).wait_recv()
                    if d + 1 < chips:
                        there, onward = towards(route + 2)

                        @pl.when(onward)
                        def _():
                            z_copy(route + 2, h, (row, there * CORES + core)).start()

                    k = lax.rem(came + chips - chip, chips) - 1
                    for t in range(1, rows):
                        take(raw[route, h], staged.at[k, h, t - 1], t)
                        spread(row, came, h, t, row_peers[rows - t - 1]).start()
                    take(raw[route, h], kept.at[came, band(row, h), :], 0)

    def multiply(d):
        for route in range(len(routes)):
            if routes[route][0] != d:
                continue
            came, valid = origin(route)

            @pl.when(valid)
            def _():
                for h in range(SPLIT):
                    for t in range(1, rows):
                        source_row = lax.rem(row + t, rows)
                        spread(source_row, came, h, t, row_peers[0]).wait_recv()
                product(came)

    for d in range(1, chips):
        pass_on(d)
        if d == 1:
            bring.wait()
            swap.wait()
            product(chip)
        else:
            multiply(d - 1)
    multiply(chips - 1)

    for route in range(len(routes)):
        there, sent = towards(route)
        came, valid = origin(route)
        for h in range(SPLIT):

            @pl.when(sent)
            def _():
                z_copy(route, h, (row, there * CORES + core)).wait_send()

            @pl.when(valid)
            def _():
                for t in range(1, rows):
                    spread(row, came, h, t, row_peers[rows - t - 1]).wait_send()

    for came in range(chips):
        keep(came).wait()
        for k in range(1, total):
            handout(came, k).wait_send()
            other, device = place(total - k)
            remote(
                ready.at[came, me],
                out_ref.at[other, :, came],
                x_send.at[came, k],
                x_recv.at[came, k],
                device,
            ).wait_recv()


def halves_by_part(integrals, ids, coefficients, rows, orbs, blocks, count):
    chips = orbs // CORES
    orb_local, basis = coefficients.shape
    aux_local, local_rows, _ = integrals.shape
    tile = local_rows // blocks
    total = rows * chips
    part = orb_local // total
    piece = orb_local // rows // SPLIT
    routes = 2 * (chips - 1)
    dtype = coefficients.dtype
    scratch = [
        pltpu.VMEM((basis // tile, piece, tile), dtype) for _ in range(routes * SPLIT)
    ]
    scratch += [
        pltpu.VMEM((basis // tile, orb_local, tile), dtype),
        pltpu.VMEM((basis // tile, orb_local // rows, tile), dtype),
        pltpu.VMEM((chips, orb_local, count * tile), dtype),
        pltpu.VMEM((chips - 1, SPLIT, rows - 1, piece, count * tile), dtype),
        pltpu.VMEM((CORES,) + integrals.shape, dtype),
        pltpu.VMEM((chips, total, CORES * aux_local, part, local_rows), dtype),
        pltpu.VMEM((rows, 1, ids.shape[1]), jnp.int32),
        pltpu.SMEM((rows, 1, ids.shape[1]), jnp.int32),
        pltpu.SemaphoreType.DMA((routes, SPLIT)),
        pltpu.SemaphoreType.DMA((routes, SPLIT)),
        pltpu.SemaphoreType.DMA((chips - 1, SPLIT, rows)),
        pltpu.SemaphoreType.DMA((chips - 1, SPLIT, rows)),
        pltpu.SemaphoreType.DMA((4,)),
        pltpu.SemaphoreType.DMA((rows,)),
        pltpu.SemaphoreType.DMA((rows,)),
        pltpu.SemaphoreType.DMA((chips, total)),
        pltpu.SemaphoreType.DMA((chips, total)),
    ]
    dims = (rows, chips, orb_local, tile, count, aux_local, blocks, part)
    return pl.pallas_call(
        functools.partial(halves_kernel, dims),
        out_shape=jax.ShapeDtypeStruct(
            (total, CORES * aux_local, chips, part, local_rows), dtype
        ),
        in_specs=[pl.BlockSpec(memory_space=pltpu.VMEM)]
        + [pl.BlockSpec(memory_space=pl.ANY)] * 2,
        out_specs=pl.BlockSpec(memory_space=pl.ANY),
        scratch_shapes=scratch,
        compiler_params=pltpu.CompilerParams(
            collective_id=0, has_side_effects=True, vmem_limit_bytes=60 << 20
        ),
    )(ids, coefficients, integrals)


def finish_kernel(rows, chips, gram_ref, all_ref, out_ref, *scratch):
    part0, sum0, part1, sum1, part2, share, full, coef_ref = scratch[:8]
    send0, recv0, send1, recv1, send2, recv2, send3, recv3, l_sem = scratch[8:]
    window = pltpu.make_async_copy(
        all_ref.at[:, pl.ds(0, coef_ref.shape[1])], coef_ref, l_sem
    )
    window.start()
    row = lax.axis_index("row")
    orb = lax.axis_index("orb")
    chip = orb // CORES
    core = orb % CORES
    height = share.shape[0]
    half = height * chips
    partner = (row, chip * CORES + 1 - core)
    row_peers = [lax.rem(row + t, rows) for t in range(1, rows)]
    chip_peers = [lax.rem(chip + t, chips) for t in range(1, chips)]
    greet(
        [partner]
        + [(peer, orb) for peer in row_peers]
        + [(row, peer * CORES + core) for peer in chip_peers]
    )
    order = row_peers + [row]
    first = []
    for t, peer in enumerate(order):
        first.append(
            remote(
                gram_ref.at[peer, 1 - core], part0.at[peer], send0.at[t], recv0.at[t], partner
            )
        )
        first[-1].start()
    second = []
    for t, peer in enumerate(order):
        first[t].wait_recv()
        total = gram_ref[peer, core].astype(jnp.float32) + part0[peer].astype(jnp.float32)
        sum0[peer] = total.astype(sum0.dtype)
        if t < rows - 1:
            second.append(
                remote(sum0.at[peer], part1.at[t], send1.at[t], recv1.at[t], (peer, orb))
            )
            second[-1].start()
    for copy in second:
        copy.wait_recv()
    total = sum0[row].astype(jnp.float32)
    for t in range(rows - 1):
        total = total + part1[t].astype(jnp.float32)
    sum1[...] = total.astype(sum1.dtype).reshape(sum1.shape)
    third = []
    for t, peer in enumerate(chip_peers):
        device = (row, peer * CORES + core)
        third.append(remote(sum1.at[peer], part2.at[t], send2.at[t], recv2.at[t], device))
        third[-1].start()
    for copy in third:
        copy.wait_recv()
    total = sum1[chip].astype(jnp.float32)
    for t in range(chips - 1):
        total = total + part2[t].astype(jnp.float32)
    share[...] = total.astype(share.dtype)

    def block(from_core, from_chip):
        start = pl.multiple_of(from_core * half + from_chip * height, height)
        return full.at[pl.ds(start, height), :]

    fourth = [
        remote(share, block(core, chip), send3.at[0, 0], recv3.at[0, 0], partner)
    ]
    for t, peer in enumerate(chip_peers):
        device = (row, peer * CORES + core)
        fourth.append(
            remote(share, block(core, chip), send3.at[0, t + 1], recv3.at[0, t + 1], device)
        )
    for copy in fourth:
        copy.start()
    full[pl.ds(pl.multiple_of(core * half + chip * height, height), height), :] = share[...]
    passed = []
    for t in range(1, chips):
        source = lax.rem(chip + chips - t, chips)
        remote(
            share, block(core, source), send3.at[0, t], recv3.at[0, t], partner
        ).wait_recv()
        passed.append(
            remote(
                block(core, source),
                block(core, source),
                send3.at[1, t],
                recv3.at[1, t],
                partner,
            )
        )
        passed[-1].start()
    mine = pl.ds(pl.multiple_of(core * half, half), half)
    theirs = pl.ds(pl.multiple_of((1 - core) * half, half), half)
    window.wait()
    result = jnp.dot(coef_ref[:, mine], full[mine, :], preferred_element_type=jnp.float32)
    remote(share, block(1 - core, chip), send3.at[0, 0], recv3.at[0, 0], partner).wait_recv()
    for t in range(1, chips):
        source = lax.rem(chip + chips - t, chips)
        remote(
            block(core, source), block(1 - core, source), send3.at[1, t], recv3.at[1, t], partner
        ).wait_recv()
    out_ref[...] = result + jnp.dot(
        coef_ref[:, theirs], full[theirs, :], preferred_element_type=jnp.float32
    )
    for copy in first + second + third + fourth + passed:
        copy.wait_send()


def finish(gram, coefs, rows, chips):
    width = gram.shape[-1]
    half = gram.shape[2]
    height = half // chips
    dtype = gram.dtype
    return pl.pallas_call(
        functools.partial(finish_kernel, rows, chips),
        out_shape=jax.ShapeDtypeStruct((coefs.shape[0], width), jnp.float32),
        in_specs=[
            pl.BlockSpec(memory_space=pltpu.VMEM),
            pl.BlockSpec(memory_space=pl.ANY),
        ],
        out_specs=pl.BlockSpec(memory_space=pltpu.VMEM),
        scratch_shapes=[
            pltpu.VMEM((rows, half, width), dtype),
            pltpu.VMEM((rows, half, width), dtype),
            pltpu.VMEM((rows - 1, half, width), dtype),
            pltpu.VMEM((chips, height, width), dtype),
            pltpu.VMEM((chips - 1, height, width), dtype),
            pltpu.VMEM((height, width), dtype),
            pltpu.VMEM((CORES * half, width), dtype),
            pltpu.VMEM((coefs.shape[0], CORES * half), dtype),
            pltpu.SemaphoreType.DMA((rows,)),
            pltpu.SemaphoreType.DMA((rows,)),
            pltpu.SemaphoreType.DMA((rows,)),
            pltpu.SemaphoreType.DMA((rows,)),
            pltpu.SemaphoreType.DMA((chips,)),
            pltpu.SemaphoreType.DMA((chips,)),
            pltpu.SemaphoreType.DMA((CORES, chips)),
            pltpu.SemaphoreType.DMA((CORES, chips)),
            pltpu.SemaphoreType.DMA,
        ],
        compiler_params=pltpu.CompilerParams(collective_id=2, has_side_effects=True),
    )(gram, coefs)


def per_device(rows, orbs, integrals, tile_ids, coefficients, metric):
    aux_local, local_rows, kept_width = integrals.shape
    orb_local, basis_width = coefficients.shape
    block_count, kept_count = tile_ids.shape
    if orb_local % (16 * SPLIT * rows) or orb_local * CORES % (8 * rows * orbs) or block_count * kept_count % 8:
        return plain_device(rows, orbs, integrals, tile_ids, coefficients, metric)
    chips = orbs // CORES
    aux = aux_local * orbs
    window = local_rows * rows
    count = block_count * kept_count
    held = chips * orb_local
    part = held // (rows * chips)
    lanes = -(-count // 128) * 128
    ids = jnp.pad(tile_ids.reshape(1, count), ((0, 0), (0, lanes - count)))
    by_part = halves_by_part(integrals, ids, coefficients, rows, orbs, block_count, count)
    by_part = by_part.reshape(rows, aux, part, local_rows)
    core = lax.axis_index("orb") % CORES
    order = metric.reshape(chips, CORES, aux_local, chips, CORES, aux_local)
    order = jnp.where(core == 0, order, order[:, ::-1, :, :, ::-1, :]).reshape(aux, aux)
    mixed = jnp.einsum(
        "pq,rpjm->rqjm", order, by_part.astype(jnp.float32), precision=lax.Precision.HIGHEST
    ).astype(jnp.bfloat16)
    gram = jnp.einsum(
        "rqjm,sqjn->srmn", by_part, mixed, preferred_element_type=jnp.float32
    ).astype(jnp.bfloat16)
    gram = gram.reshape(rows, CORES, window // CORES, local_rows)
    return finish(gram, coefficients, rows, chips)


def plain_device(rows, orbs, integrals, tile_ids, coefficients, metric):
    aux_local, local_rows, kept_width = integrals.shape
    orb_local, basis_width = coefficients.shape
    block_count, kept_count = tile_ids.shape
    tile_rows = local_rows // block_count
    orbitals = orb_local * orbs
    aux = aux_local * orbs
    window = local_rows * rows
    part = orbitals // (rows * orbs)
    picked = pick(coefficients, tile_ids.reshape(block_count * kept_count), tile_rows)
    col_piece = lax.all_gather(picked, "orb", axis=0, tiled=True)
    slabs = integrals.reshape(aux_local, block_count, tile_rows, kept_width)
    halves = [
        jnp.einsum(
            "pmk,jk->pjm",
            slabs[:, b],
            col_piece[:, b * kept_width : (b + 1) * kept_width],
            preferred_element_type=jnp.float32,
        ).astype(jnp.bfloat16)
        for b in range(block_count)
    ]
    halves = jnp.concatenate(halves, axis=2)
    outgoing = halves.reshape(aux_local, rows * orbs, part, local_rows).transpose(1, 0, 2, 3)
    by_part = lax.all_to_all(outgoing, ("row", "orb"), split_axis=0, concat_axis=0, tiled=True)
    by_part = by_part.reshape(rows, aux, part, local_rows)
    mixed = jnp.einsum(
        "pq,rpjm->rqjm", metric, by_part.astype(jnp.float32), precision=lax.Precision.HIGHEST
    ).astype(jnp.bfloat16)
    gram = jnp.einsum(
        "rqjm,sqjn->rmsn", by_part, mixed, preferred_element_type=jnp.float32
    ).astype(jnp.bfloat16)
    gram = gram.reshape(orbs, window // orbs, rows, local_rows).transpose(2, 0, 1, 3)
    gram = gram.reshape(rows * window, local_rows)
    share = lax.psum_scatter(gram, ("row", "orb"), scatter_dimension=0, tiled=True)
    columns = lax.all_gather(share, "orb", axis=0, tiled=True)
    return jnp.dot(coefficients[:, :window], columns, preferred_element_type=jnp.float32)


def solution(mesh):
    return jax.shard_map(
        functools.partial(per_device, mesh.shape["row"], mesh.shape["orb"]),
        mesh=mesh,
        in_specs=(P("orb", "row", None), P("row", None), P("orb", None), P()),
        out_specs=P("orb", "row"),
        check_vma=False,
    )
```
